32 devices in a mesh: ctx: 4 (over z), fsdp: 8 (over y, x, core).
Axes of the slice: x: 2, y: 2, z: 4, core: 2. Of those that a mesh axis runs over, the one named last changes fastest.
Arguments:
- hidden_in: bfloat16 [8, 512, 1536], P('fsdp', 'ctx'), may hold values from -6 to 6
- out_grad: bfloat16 [8, 512, 1536], P('fsdp', 'ctx'), may hold values from -6 to 6
- attn_gain: bfloat16 [1536], P('fsdp'), may hold values from 0.099609375 to 1.8984375
- ffn_gain: bfloat16 [1536], P('fsdp'), may hold values from 0.099609375 to 1.8984375
- w_query: bfloat16 [1536, 1536], P('fsdp')
- w_key: bfloat16 [1536, 512], P('fsdp'), may hold values from -0.15625 to 0.15625
- w_value: bfloat16 [1536, 512], P('fsdp'), may hold values from -0.15625 to 0.15625
- w_output: bfloat16 [1536, 1536], P('fsdp'), may hold values from -0.625 to 0.625
- w_router: bfloat16 [1536, 40], P('fsdp')
- w_gate: bfloat16 [40, 1536, 512], P('ctx', 'fsdp'), may hold values from -0.15625 to 0.15625
- w_up: bfloat16 [40, 1536, 512], P('ctx', 'fsdp'), may hold values from -0.15625 to 0.15625
- w_down: bfloat16 [40, 512, 1536], P('ctx', 'fsdp'), may hold values from -0.25 to 0.25
- expert_ids: int32 [8, 512, 8], P('fsdp', 'ctx'), may hold values from 0 to 39, all different within a row; in each aligned block of 128 rows (0 to 127, 128 to 255, ..., all dimensions but the last counted through in order) at most 32 rows name the same one
Outputs:
- block_out: bfloat16 [8, 512, 1536], P('fsdp', 'ctx')
- in_grad: float32 [8, 512, 1536], P('fsdp', 'ctx')
- attn_gain_grad: float32 [1536], P(('ctx', 'fsdp'))
- ffn_gain_grad: float32 [1536], P(('ctx', 'fsdp'))
- query_grad: float32 [1536, 1536], P(('ctx', 'fsdp'))
- key_grad: float32 [1536, 512], P(('ctx', 'fsdp'))
- value_grad: float32 [1536, 512], P(('ctx', 'fsdp'))
- output_grad: float32 [1536, 1536], P(('ctx', 'fsdp'))
- router_grad: float32 [1536, 40], P(('ctx', 'fsdp'))
- gate_grad: float32 [40, 1536, 512], P('ctx', 'fsdp')
- up_grad: float32 [40, 1536, 512], P('ctx', 'fsdp')
- down_grad: float32 [40, 512, 1536], P('ctx', 'fsdp')
The draws below stay inside these ranges and needn't reach their ends.
Inputs may be any that keep to these rules, and one draw needn't show every extreme that they name: `expert_ids`: in the rows of one device (128 tokens) each token names 8 different experts, no expert is named by more than 32 of those tokens, a bound that some block reaches.
All inputs are finite; a program needn't handle non-finite values.
Results may differ from the reference program's by a relative error of at most 0.017.
Values may be sent and summed in bfloat16 or wider, within the bound.
No kernel may reach another device: no remote copies, remote signals or barrier semaphores. Data moves between devices by JAX's collectives and lax.ppermute only.
A program may use at most 256 MiB of HBM per device.

```python
import math
import jax
import jax.numpy as jnp
import numpy as np
from jax import lax

D = 1536
H = 24
KVH = 8
HD = 64
E = 40
F = 512
TOP = 8
BLK = 64
CAP = 32
SEQ_LEN = 512
SEQS = 8
N_CTX = 4


def draw_w_query(key, part):
    base_key = jax.random.fold_in(key, 11)
    values = jax.random.normal(base_key, (D, H * HD), jnp.float32) * D ** (-0.5)
    return values.astype(jnp.bfloat16)


def draw_w_router(key, part):
    base_key = jax.random.fold_in(key, 23)
    values = jax.random.normal(base_key, (D, E), jnp.float32) * D ** (-0.5)
    return values.astype(jnp.bfloat16)


def level_of(rng, dims, cuts, least, top_value):
    loudness, own = 1.0, jax.random.fold_in(rng, 6)
    for axis_at, blocks in cuts:
        heights = jnp.exp(jax.random.uniform(jax.random.fold_in(own, axis_at), (blocks,), jnp.float32, least / len(cuts), top_value / len(cuts)))
        loudness = loudness * jnp.repeat(heights, dims[axis_at] // blocks).reshape([-1 if axis == axis_at else 1 for axis in range(len(dims))])
    return loudness


def deal_out(own_key, own, number, rows, amount, top, bound, slope):
    ranking = jax.random.permutation(own_key, amount)
    crowded, usual = portions_of(amount, rows * top, bound, slope, True), portions_of(amount, rows * top, bound, slope, False)
    places = jnp.arange(amount)

    def named(lengths, rotation):
        used = int((lengths > 0).sum())
        fixed = max(1, used // 4)
        passed = fixed + (places - fixed + rotation * (used - fixed)) % max(1, amount - fixed)
        return jnp.zeros((amount,), jnp.int32).at[ranking[jnp.where(places < fixed, places, passed)]].set(jnp.asarray(lengths, jnp.int32))

    lengths = jnp.where(number % 4 == 0, named(crowded, number // 4), named(usual, number - number // 4 - 1))
    mixed = jax.random.permutation(jax.random.fold_in(own, 3), amount)
    source_of, taker = mixed[0:amount // 2 * 2:2], mixed[1:amount // 2 * 2:2]
    slack = jnp.minimum(lengths[source_of] - 1, bound - lengths[taker]) // 2
    slack = jnp.where((source_of == ranking[0]) | (taker == ranking[0]) | (lengths[taker] == 0), 0, jnp.maximum(slack, 0))
    passed = jax.random.randint(jax.random.fold_in(own, 4), (amount // 2,), 0, 1 << 20) % (slack + 1)
    lengths = lengths.at[source_of].add(-passed).at[taker].add(passed)
    members = jnp.searchsorted(jnp.cumsum(lengths), jnp.arange(rows * top), side="right").astype(jnp.int32)
    table = members.reshape(top, rows).T
    table = table[jax.random.permutation(jax.random.fold_in(own, 1), rows)]
    rotation = jax.random.randint(jax.random.fold_in(own, 2), (rows, 1), 0, top)
    return jnp.take_along_axis(table, (jnp.arange(top)[None, :] + rotation) % top, axis=1)


def portions_of(number_of, total, most, slope, full):
    loads = [(1 << 20) // math.isqrt(grade ** slope) + 1 for grade in range(1, number_of + 1)]
    largest = most if full else min(most, max(-(-total // number_of), total * loads[0] // sum(loads)))
    least = 1 if total - largest >= number_of - 1 else 0
    holding, surplus = [largest] + [least] * (number_of - 1), total - largest - least * (number_of - 1)
    while surplus > 0:
        free = [i for i in range(1, number_of) if holding[i] < largest] or [i for i in range(1, number_of) if holding[i] < most]
        whole, budget = sum([loads[i] for i in free]), surplus
        for i in free:
            extra = min(most - holding[i], max(1, budget * loads[i] // whole), surplus)
            holding[i] = holding[i] + extra
            surplus = surplus - extra
    return np.array(holding)


def gaussian(stream_key, shape, deviation, bound, shards=(), kind=jnp.bfloat16):
    array = deviation * jax.random.normal(stream_key, shape, jnp.float32)
    if shards:
        array = array * level_of(stream_key, shape, shards, -0.22, 0.18)
    return jnp.clip(array, -bound, bound).astype(kind)


def setup_inputs(seed: int = 0) -> dict:
    key_list = jax.random.split(jax.random.key(seed), 14)
    hidden_in = gaussian(key_list[0], (SEQS, SEQ_LEN, D), 1.0, 6.0, ((0, 8), (1, 4)))
    out_grad = gaussian(key_list[1], (SEQS, SEQ_LEN, D), 1.0, 6.0, ((0, 8), (1, 4)))
    attn_gain = jnp.clip(1.0 + 0.18 * jax.random.normal(key_list[2], (D,), jnp.float32), 0.099609375, 1.8984375).astype(jnp.bfloat16)
    ffn_gain = jnp.clip(1.0 + 0.18 * jax.random.normal(key_list[3], (D,), jnp.float32), 0.099609375, 1.8984375).astype(jnp.bfloat16)
    w_query = draw_w_query(jax.random.fold_in(key_list[13], 71), 0)
    w_key = gaussian(key_list[5], (D, KVH * HD), D ** -0.5, 0.15625, ((0, 8),))
    w_value = gaussian(key_list[6], (D, KVH * HD), D ** -0.5, 0.15625, ((0, 8),))
    w_output = gaussian(key_list[7], (H * HD, D), (H * HD // 16) ** -0.5, 0.625, ((0, 8),))
    w_router = draw_w_router(jax.random.fold_in(key_list[13], 71), 0)
    w_gate = gaussian(key_list[9], (E, D, F), D ** -0.5, 0.15625, ((0, 4), (1, 8)))
    w_up = gaussian(key_list[10], (E, D, F), D ** -0.5, 0.15625, ((0, 4), (1, 8)))
    w_down = gaussian(key_list[11], (E, F, D), F ** -0.5, 0.25, ((0, 4), (1, 8)))
    expert_ids_keys = jax.random.split(jax.random.fold_in(key_list[12], 1), SEQS * SEQ_LEN // (2 * BLK))
    expert_ids_turns = jax.random.permutation(jax.random.fold_in(key_list[12], 3), SEQS * SEQ_LEN // (2 * BLK))
    expert_ids = jax.vmap(lambda own, number: deal_out(jax.random.fold_in(key_list[12], 2), own, number, 2 * BLK, E, TOP, CAP, 1))(expert_ids_keys, expert_ids_turns).reshape((SEQS, SEQ_LEN, TOP))
    return {"hidden_in": hidden_in, "out_grad": out_grad, "attn_gain": attn_gain, "ffn_gain": ffn_gain, "w_query": w_query, "w_key": w_key, "w_value": w_value, "w_output": w_output, "w_router": w_router, "w_gate": w_gate, "w_up": w_up, "w_down": w_down, "expert_ids": expert_ids}


EPS = 1e-05
ROPE_BASE = 10000.0
NEG_FILL = -1e+30

def round_trip(values):
    return lax.optimization_barrier(values.astype(jnp.bfloat16)).astype(jnp.float32)

def rms_scale(values, gain_vec):
    inverse = lax.rsqrt(lax.optimization_barrier(jnp.mean(values * values, axis=-1, keepdims=True)) + EPS)
    return values * inverse * gain_vec

def mirrored_positions(count_rows, half_rows, ctx_count):
    row_index = jnp.arange(count_rows, dtype=jnp.int32)
    device_row = row_index // (2 * half_rows)
    within = row_index % (2 * half_rows)
    return jnp.where(within < half_rows, device_row * half_rows + within, (2 * ctx_count - 1 - device_row) * half_rows + within - half_rows)

def rope_tables(positions, head_size):
    half_size = head_size // 2
    freq_row = ROPE_BASE ** (-(jnp.arange(half_size, dtype=jnp.float32) * 2.0) / head_size)
    angles = positions.astype(jnp.float32)[:, None] * freq_row[None, :]
    return (jnp.cos(angles)[:, None, :], jnp.sin(angles)[:, None, :])

def rotate(values, cos_table, sin_table):
    half_size = values.shape[-1] // 2
    first_half = values[..., :half_size]
    second_half = values[..., half_size:]
    return jnp.concatenate([first_half * cos_table - second_half * sin_table, second_half * cos_table + first_half * sin_table], axis=-1)

def unrotate(values, cos_table, sin_table):
    half_size = values.shape[-1] // 2
    first_half = values[..., :half_size]
    second_half = values[..., half_size:]
    return jnp.concatenate([first_half * cos_table + second_half * sin_table, second_half * cos_table - first_half * sin_table], axis=-1)

def block_scores(query_piece, key_wide, key_pos, query_pos, score_scale):
    raw_scores = jnp.einsum('rkgd,ckd->kgrc', query_piece, key_wide) * score_scale
    causal_mask = key_pos[None, :] <= query_pos[:, None]
    return jnp.where(causal_mask[None, None], raw_scores, NEG_FILL)

def add_pair(first_term, second_term):
    return first_term + second_term

def reference(hidden_in, out_grad, attn_gain, ffn_gain, w_query, w_key, w_value, w_output, w_router, w_gate, w_up, w_down, expert_ids):
    seq_len = 2 * BLK * N_CTX
    group_size = H // KVH
    score_scale = HD ** (-0.5)
    query_block = min(512, seq_len)
    query_blocks = seq_len // query_block
    gain_attn = attn_gain.astype(jnp.float32)
    gain_ffn = ffn_gain.astype(jnp.float32)
    gate_wide = w_gate.astype(jnp.float32)
    up_wide = w_up.astype(jnp.float32)
    down_wide = w_down.astype(jnp.float32)
    positions = mirrored_positions(seq_len, BLK, N_CTX)
    cos_table, sin_table = rope_tables(positions, HD)
    expert_range = jnp.arange(E, dtype=jnp.int32)
    block_index = jnp.arange(N_CTX, dtype=jnp.int32)[:, None]
    block_ids = jnp.arange(query_blocks, dtype=jnp.int32)

    def one_sequence(grads_in, inputs):
        x_seq, dy_seq, route_seq = inputs
        x_rows = x_seq.astype(jnp.float32)
        normed_one = rms_scale(x_rows, gain_attn).astype(jnp.bfloat16)
        query_rot = round_trip(rotate(jnp.dot(normed_one, w_query, preferred_element_type=jnp.float32).reshape(seq_len, H, HD), cos_table, sin_table))
        key_wide = round_trip(rotate(jnp.dot(normed_one, w_key, preferred_element_type=jnp.float32).reshape(seq_len, KVH, HD), cos_table, sin_table))
        value_wide = round_trip(jnp.dot(normed_one, w_value, preferred_element_type=jnp.float32)).reshape(seq_len, KVH, HD)
        query_four = query_rot.reshape(seq_len, KVH, group_size, HD)

        def forward_block(block_id):
            start = block_id * query_block
            query_piece = lax.dynamic_slice_in_dim(query_four, start, query_block, 0)
            query_pos = lax.dynamic_slice_in_dim(positions, start, query_block, 0)
            scores = block_scores(query_piece, key_wide, positions, query_pos, score_scale)
            row_top = lax.optimization_barrier(jnp.max(scores, axis=-1))
            log_total = row_top + jnp.log(lax.optimization_barrier(jnp.sum(jnp.exp(scores - row_top[..., None]), axis=-1)))
            weights = round_trip(jnp.exp(scores - log_total[..., None]))
            attended = jnp.einsum('kgrc,ckd->rkgd', weights, value_wide)
            return (attended, log_total)
        attended, log_totals = lax.map(forward_block, block_ids)
        attn_rows = attended.reshape(seq_len, H * HD).astype(jnp.bfloat16)
        log_total_all = log_totals.transpose(1, 2, 0, 3).reshape(KVH, group_size, seq_len)
        mid_rows = x_rows + jnp.dot(attn_rows, w_output, preferred_element_type=jnp.float32)
        normed_two = rms_scale(mid_rows, gain_ffn).astype(jnp.bfloat16)
        logits = jnp.dot(normed_two, w_router, preferred_element_type=jnp.float32)
        route_hot = (route_seq[..., None] == expert_range).astype(jnp.float32)
        chosen = lax.optimization_barrier(jnp.sum(route_hot * logits[:, None, :], axis=-1))
        gates = jax.nn.softmax(chosen, axis=-1)
        flat_routes = route_seq.reshape(N_CTX, 2 * BLK * TOP)
        route_count = (flat_routes[..., None] == expert_range).astype(jnp.int32)
        slot_index = lax.optimization_barrier(jnp.sum((jnp.cumsum(route_count, axis=1) - 1) * route_count, axis=-1))

        def to_experts(rows_in):
            buffer = jnp.zeros((N_CTX, E, CAP, D), rows_in.dtype).at[block_index, flat_routes, slot_index].set(rows_in)
            return buffer.transpose(1, 0, 2, 3).reshape(E, N_CTX * CAP, D)

        def from_experts(buffer):
            grid = buffer.reshape(E, N_CTX, CAP, D).transpose(1, 0, 2, 3)
            return grid[block_index, flat_routes, slot_index].reshape(seq_len, TOP, D)
        repeated = jnp.broadcast_to(normed_two[:, None, :], (seq_len, TOP, D)).reshape(N_CTX, 2 * BLK * TOP, D)
        expert_in = to_experts(repeated).astype(jnp.float32)
        gate_pre = jnp.einsum('ecd,edf->ecf', expert_in, gate_wide)
        up_pre = jnp.einsum('ecd,edf->ecf', expert_in, up_wide)
        sigma = jax.nn.sigmoid(gate_pre)
        silu_val = gate_pre * sigma
        hidden_e = round_trip(silu_val * up_pre)
        expert_out = jnp.einsum('ecf,efd->ecd', hidden_e, down_wide).astype(jnp.bfloat16)
        out_rows = from_experts(expert_out).astype(jnp.float32)
        mixture = lax.optimization_barrier(jnp.sum(gates[..., None] * out_rows, axis=1))
        block_out = (mid_rows + mixture).astype(jnp.bfloat16)
        grad_rows = dy_seq.astype(jnp.float32)
        gate_grad_k = lax.optimization_barrier(jnp.sum(out_rows * grad_rows[:, None, :], axis=-1))
        d_rows_out = (gates[..., None] * grad_rows[:, None, :]).astype(jnp.bfloat16).reshape(N_CTX, 2 * BLK * TOP, D)
        d_expert_out = to_experts(d_rows_out).astype(jnp.float32)
        d_hidden = jnp.einsum('ecd,efd->ecf', d_expert_out, down_wide)
        down_step = jnp.einsum('ecf,ecd->efd', hidden_e, d_expert_out)
        d_silu = sigma * (1.0 + gate_pre * (1.0 - sigma))
        d_gate_pre = round_trip(d_hidden * up_pre * d_silu)
        d_up_pre = round_trip(d_hidden * silu_val)
        gate_step = jnp.einsum('ecd,ecf->edf', expert_in, d_gate_pre)
        up_step = jnp.einsum('ecd,ecf->edf', expert_in, d_up_pre)
        d_expert_in = (jnp.einsum('ecf,edf->ecd', d_gate_pre, gate_wide) + jnp.einsum('ecf,edf->ecd', d_up_pre, up_wide)).astype(jnp.bfloat16)
        d_normed_two = lax.optimization_barrier(jnp.sum(from_experts(d_expert_in).astype(jnp.float32), axis=1))
        gate_mean = lax.optimization_barrier(jnp.sum(gates * gate_grad_k, axis=-1, keepdims=True))
        d_chosen = gates * (gate_grad_k - gate_mean)
        d_logits = lax.optimization_barrier(jnp.sum(route_hot * d_chosen[..., None], axis=1)).astype(jnp.bfloat16)
        router_step = jnp.dot(normed_two.T, d_logits, preferred_element_type=jnp.float32)
        d_normed_two = d_normed_two + jnp.dot(d_logits, w_router.T, preferred_element_type=jnp.float32)
        _, norm_two_back = jax.vjp(rms_scale, mid_rows, gain_ffn)
        d_mid_norm, gain_ffn_step = norm_two_back(d_normed_two)
        d_mid = grad_rows + d_mid_norm
        d_proj = d_mid.astype(jnp.bfloat16)
        output_step = jnp.dot(attn_rows.T, d_proj, preferred_element_type=jnp.float32)
        d_attn = jnp.dot(d_proj, w_output.T, preferred_element_type=jnp.float32).astype(jnp.bfloat16)
        d_attn_four = d_attn.astype(jnp.float32).reshape(seq_len, KVH, group_size, HD)
        attn_four = attn_rows.astype(jnp.float32).reshape(seq_len, KVH, group_size, HD)
        delta_all = lax.optimization_barrier(jnp.sum(d_attn_four * attn_four, axis=-1)).transpose(1, 2, 0)

        def backward_block(kv_grads, block_id):
            key_sum, value_sum = kv_grads
            start = block_id * query_block
            query_piece = lax.dynamic_slice_in_dim(query_four, start, query_block, 0)
            query_pos = lax.dynamic_slice_in_dim(positions, start, query_block, 0)
            d_piece = lax.dynamic_slice_in_dim(d_attn_four, start, query_block, 0)
            delta_piece = lax.dynamic_slice_in_dim(delta_all, start, query_block, 2)
            log_piece = lax.dynamic_slice_in_dim(log_total_all, start, query_block, 2)
            scores = block_scores(query_piece, key_wide, positions, query_pos, score_scale)
            weights = jnp.exp(scores - log_piece[..., None])
            weights_low = round_trip(weights)
            value_sum = value_sum + jnp.einsum('kgrc,rkgd->ckd', weights_low, d_piece)
            d_weights = jnp.einsum('rkgd,ckd->kgrc', d_piece, value_wide)
            d_scores = round_trip(weights * (d_weights - delta_piece[..., None]) * score_scale)
            d_query = jnp.einsum('kgrc,ckd->rkgd', d_scores, key_wide)
            key_sum = key_sum + jnp.einsum('kgrc,rkgd->ckd', d_scores, query_piece)
            return ((key_sum, value_sum), d_query)
        zeros_kv = jnp.zeros((seq_len, KVH, HD), jnp.float32)
        (key_sum, value_sum), d_query_blocks = lax.scan(backward_block, (zeros_kv, zeros_kv), block_ids)
        d_query = unrotate(d_query_blocks.reshape(seq_len, H, HD), cos_table, sin_table).reshape(seq_len, H * HD).astype(jnp.bfloat16)
        d_key = unrotate(key_sum, cos_table, sin_table).reshape(seq_len, KVH * HD).astype(jnp.bfloat16)
        d_value = value_sum.reshape(seq_len, KVH * HD).astype(jnp.bfloat16)
        query_step = jnp.dot(normed_one.T, d_query, preferred_element_type=jnp.float32)
        key_step = jnp.dot(normed_one.T, d_key, preferred_element_type=jnp.float32)
        value_step = jnp.dot(normed_one.T, d_value, preferred_element_type=jnp.float32)
        d_normed_one = jnp.dot(d_query, w_query.T, preferred_element_type=jnp.float32) + jnp.dot(d_key, w_key.T, preferred_element_type=jnp.float32) + jnp.dot(d_value, w_value.T, preferred_element_type=jnp.float32)
        _, norm_one_back = jax.vjp(rms_scale, x_rows, gain_attn)
        d_x_norm, gain_attn_step = norm_one_back(d_normed_one)
        in_grad = d_mid + d_x_norm
        step_grads = (gain_attn_step, gain_ffn_step, query_step, key_step, value_step, output_step, router_step, gate_step, up_step, down_step)
        return (jax.tree.map(add_pair, grads_in, step_grads), (block_out, in_grad))
    zero_grads = (jnp.zeros((D,), jnp.float32), jnp.zeros((D,), jnp.float32), jnp.zeros((D, H * HD), jnp.float32), jnp.zeros((D, KVH * HD), jnp.float32), jnp.zeros((D, KVH * HD), jnp.float32), jnp.zeros((H * HD, D), jnp.float32), jnp.zeros((D, E), jnp.float32), jnp.zeros((E, D, F), jnp.float32), jnp.zeros((E, D, F), jnp.float32), jnp.zeros((E, F, D), jnp.float32))
    grads, (block_out, in_grad) = lax.scan(one_sequence, zero_grads, (hidden_in, out_grad, expert_ids))
    return (block_out, in_grad, grads[0], grads[1], grads[2], grads[3], grads[4], grads[5], grads[6], grads[7], grads[8], grads[9])
```

```python
import functools

import jax
import jax.numpy as jnp
from jax import lax
from jax.experimental import pallas as pl
from jax.experimental.pallas import tpu as pltpu
from jax.sharding import PartitionSpec as P

H = 24
KVH = 8
HD = 64
E = 40
TOP = 8
CAP = 32


EPS = 1e-05
ROPE_BASE = 10000.0
NEG_FILL = -1e30


def rms_scale(values, gain_vec):
    inverse = lax.rsqrt(jnp.mean(values * values, axis=-1, keepdims=True) + EPS)
    return values * inverse * gain_vec


def mirrored_positions(count_rows, half_rows, ctx_count, first_device):
    row_index = jnp.arange(count_rows, dtype=jnp.int32)
    device_row = first_device + row_index // (2 * half_rows)
    within = row_index % (2 * half_rows)
    return jnp.where(
        within < half_rows,
        device_row * half_rows + within,
        (2 * ctx_count - 1 - device_row) * half_rows + within - half_rows,
    )


def rope_tables(positions, head_size):
    half_size = head_size // 2
    freq_row = ROPE_BASE ** (-(jnp.arange(half_size, dtype=jnp.float32) * 2.0) / head_size)
    angles = positions.astype(jnp.float32)[:, None] * freq_row[None, :]
    return (jnp.cos(angles)[:, None, :], jnp.sin(angles)[:, None, :])


def rotate(values, cos_table, sin_table):
    half_size = values.shape[-1] // 2
    first_half = values[..., :half_size]
    second_half = values[..., half_size:]
    return jnp.concatenate(
        [
            first_half * cos_table - second_half * sin_table,
            second_half * cos_table + first_half * sin_table,
        ],
        axis=-1,
    )


def unrotate(values, cos_table, sin_table):
    half_size = values.shape[-1] // 2
    first_half = values[..., :half_size]
    second_half = values[..., half_size:]
    return jnp.concatenate(
        [
            first_half * cos_table + second_half * sin_table,
            second_half * cos_table - first_half * sin_table,
        ],
        axis=-1,
    )


def block_scores(query_four, key_piece, key_pos, query_pos, score_scale):
    raw_scores = (
        jnp.einsum("rkgd,ckd->kgrc", query_four, key_piece, preferred_element_type=jnp.float32)
        * score_scale
    )
    causal_mask = key_pos[None, :] <= query_pos[:, None]
    return jnp.where(causal_mask[None, None], raw_scores, NEG_FILL)


def wide_body(
    hidden_in,
    out_grad,
    attn_gain,
    ffn_gain,
    w_query,
    w_key,
    w_value,
    w_output,
    w_router,
    w_gate,
    w_up,
    w_down,
    expert_ids,
):
    ctx_count = lax.axis_size("ctx")
    ctx_index = lax.axis_index("ctx")
    tok_rows = hidden_in.shape[1]
    half_rows = tok_rows // 2
    key_count = tok_rows * ctx_count
    key_block = min(512, key_count)
    block_count = key_count // key_block
    group_size = H // KVH
    score_scale = HD ** (-0.5)
    model_width = hidden_in.shape[2]
    layer_set = (w_query, w_key, w_value, w_output, w_router, attn_gain, ffn_gain)
    query_full, key_full, value_full, output_full, router_full, gain_one, gain_two = (
        lax.all_gather(layer_set[0], "fsdp", axis=0, tiled=True),
        lax.all_gather(layer_set[1], "fsdp", axis=0, tiled=True),
        lax.all_gather(layer_set[2], "fsdp", axis=0, tiled=True),
        lax.all_gather(layer_set[3], "fsdp", axis=0, tiled=True),
        lax.all_gather(layer_set[4], "fsdp", axis=0, tiled=True),
        lax.all_gather(layer_set[5], "fsdp", axis=0, tiled=True),
        lax.all_gather(layer_set[6], "fsdp", axis=0, tiled=True),
    )
    gate_full, up_full, down_full = (
        lax.all_gather(w_gate, "fsdp", axis=1, tiled=True),
        lax.all_gather(w_up, "fsdp", axis=1, tiled=True),
        lax.all_gather(w_down, "fsdp", axis=1, tiled=True),
    )
    x_rows = hidden_in[0].astype(jnp.float32)
    gain_attn = gain_one.astype(jnp.float32)
    gain_ffn = gain_two.astype(jnp.float32)
    normed_one = rms_scale(x_rows, gain_attn).astype(jnp.bfloat16)
    query_pos = mirrored_positions(tok_rows, half_rows, ctx_count, ctx_index)
    key_pos = mirrored_positions(key_count, half_rows, ctx_count, 0)
    cos_table, sin_table = rope_tables(query_pos, HD)
    query_rot = rotate(
        jnp.dot(normed_one, query_full, preferred_element_type=jnp.float32).reshape(
            tok_rows, H, HD
        ),
        cos_table,
        sin_table,
    ).astype(jnp.bfloat16)
    key_rot = rotate(
        jnp.dot(normed_one, key_full, preferred_element_type=jnp.float32).reshape(
            tok_rows, KVH, HD
        ),
        cos_table,
        sin_table,
    ).astype(jnp.bfloat16)
    value_rows = jnp.dot(normed_one, value_full, preferred_element_type=jnp.float32).astype(
        jnp.bfloat16
    )
    keys_all, values_all = (
        lax.all_gather(key_rot.reshape(tok_rows, KVH * HD), "ctx", axis=0, tiled=True),
        lax.all_gather(value_rows, "ctx", axis=0, tiled=True),
    )
    query_four = query_rot.reshape(tok_rows, KVH, group_size, HD)
    pos_blocks = key_pos.reshape(block_count, key_block)

    def split_blocks(flat_rows):
        return flat_rows.reshape(block_count, key_block, KVH, HD)

    def max_and_total(running, pieces):
        row_top, row_total = running
        key_piece, pos_piece = pieces
        scores = block_scores(query_four, key_piece, pos_piece, query_pos, score_scale)
        new_top = jnp.maximum(row_top, jnp.max(scores, axis=-1))
        row_total = row_total * jnp.exp(row_top - new_top) + jnp.sum(
            jnp.exp(scores - new_top[..., None]), axis=-1
        )
        return ((new_top, row_total), None)

    start_top = jnp.full((KVH, group_size, tok_rows), NEG_FILL, jnp.float32)
    start_total = jnp.zeros((KVH, group_size, tok_rows), jnp.float32)
    key_blocks = split_blocks(keys_all)
    value_blocks = split_blocks(values_all)
    (row_top, row_total), _ = lax.scan(
        max_and_total, (start_top, start_total), (key_blocks, pos_blocks)
    )
    log_total = row_top + jnp.log(row_total)

    def weigh_values(accum, pieces):
        key_piece, value_piece, pos_piece = pieces
        scores = block_scores(query_four, key_piece, pos_piece, query_pos, score_scale)
        weights = jnp.exp(scores - log_total[..., None]).astype(jnp.bfloat16)
        return (
            accum
            + jnp.einsum(
                "kgrc,ckd->rkgd", weights, value_piece, preferred_element_type=jnp.float32
            ),
            None,
        )

    accum, _ = lax.scan(
        weigh_values,
        jnp.zeros((tok_rows, KVH, group_size, HD), jnp.float32),
        (key_blocks, value_blocks, pos_blocks),
    )
    attn_rows = accum.reshape(tok_rows, H * HD).astype(jnp.bfloat16)
    mid_rows = x_rows + jnp.dot(attn_rows, output_full, preferred_element_type=jnp.float32)
    normed_two = rms_scale(mid_rows, gain_ffn).astype(jnp.bfloat16)
    logits = jnp.dot(normed_two, router_full, preferred_element_type=jnp.float32)
    route_ids = expert_ids[0]
    expert_range = jnp.arange(E, dtype=jnp.int32)
    route_hot = (route_ids[..., None] == expert_range).astype(jnp.float32)
    chosen = jnp.sum(route_hot * logits[:, None, :], axis=-1)
    gates = jax.nn.softmax(chosen, axis=-1)
    flat_routes = route_ids.reshape(tok_rows * TOP)
    route_count = (flat_routes[:, None] == expert_range).astype(jnp.int32)
    slot_index = jnp.sum((jnp.cumsum(route_count, axis=0) - 1) * route_count, axis=-1)

    def place_rows(rows_in):
        return (
            jnp.zeros((E, CAP, model_width), jnp.bfloat16).at[flat_routes, slot_index].set(rows_in)
        )

    def pick_rows(buffer):
        return buffer[flat_routes, slot_index].reshape(tok_rows, TOP, model_width)

    repeated = jnp.broadcast_to(normed_two[:, None, :], (tok_rows, TOP, model_width)).reshape(
        tok_rows * TOP, model_width
    )
    expert_in = lax.all_to_all(place_rows(repeated), "ctx", split_axis=0, concat_axis=1, tiled=True)
    gate_pre = jnp.einsum("ecd,edf->ecf", expert_in, gate_full, preferred_element_type=jnp.float32)
    up_pre = jnp.einsum("ecd,edf->ecf", expert_in, up_full, preferred_element_type=jnp.float32)
    sigma = jax.nn.sigmoid(gate_pre)
    silu_val = gate_pre * sigma
    hidden_e = (silu_val * up_pre).astype(jnp.bfloat16)
    expert_out = jnp.einsum(
        "ecf,efd->ecd", hidden_e, down_full, preferred_element_type=jnp.float32
    ).astype(jnp.bfloat16)
    returned = lax.all_to_all(expert_out, "ctx", split_axis=1, concat_axis=0, tiled=True)
    out_rows = pick_rows(returned)
    mixture = jnp.einsum("rk,rkd->rd", gates, out_rows.astype(jnp.float32))
    block_out = (mid_rows + mixture).astype(jnp.bfloat16)
    query_back, key_back, value_back, output_back, router_back, gain_one_back, gain_two_back = (
        lax.all_gather(layer_set[0], "fsdp", axis=0, tiled=True),
        lax.all_gather(layer_set[1], "fsdp", axis=0, tiled=True),
        lax.all_gather(layer_set[2], "fsdp", axis=0, tiled=True),
        lax.all_gather(layer_set[3], "fsdp", axis=0, tiled=True),
        lax.all_gather(layer_set[4], "fsdp", axis=0, tiled=True),
        lax.all_gather(layer_set[5], "fsdp", axis=0, tiled=True),
        lax.all_gather(layer_set[6], "fsdp", axis=0, tiled=True),
    )
    gate_back, up_back, down_back = (
        lax.all_gather(w_gate, "fsdp", axis=1, tiled=True),
        lax.all_gather(w_up, "fsdp", axis=1, tiled=True),
        lax.all_gather(w_down, "fsdp", axis=1, tiled=True),
    )
    keys_back, values_back = (
        lax.all_gather(key_rot.reshape(tok_rows, KVH * HD), "ctx", axis=0, tiled=True),
        lax.all_gather(value_rows, "ctx", axis=0, tiled=True),
    )
    grad_rows = out_grad[0].astype(jnp.float32)
    gate_grad_k = jnp.einsum(
        "rkd,rd->rk", out_rows, out_grad[0], preferred_element_type=jnp.float32
    )
    d_rows_out = (
        (gates[..., None] * grad_rows[:, None, :])
        .astype(jnp.bfloat16)
        .reshape(tok_rows * TOP, model_width)
    )
    d_expert_out = lax.all_to_all(
        place_rows(d_rows_out), "ctx", split_axis=0, concat_axis=1, tiled=True
    )
    d_hidden = jnp.einsum(
        "ecd,efd->ecf", d_expert_out, down_back, preferred_element_type=jnp.float32
    )
    down_local = jnp.einsum(
        "ecf,ecd->efd", hidden_e, d_expert_out, preferred_element_type=jnp.float32
    )
    d_silu = sigma * (1.0 + gate_pre * (1.0 - sigma))
    d_gate_pre = (d_hidden * up_pre * d_silu).astype(jnp.bfloat16)
    d_up_pre = (d_hidden * silu_val).astype(jnp.bfloat16)
    gate_local = jnp.einsum(
        "ecd,ecf->edf", expert_in, d_gate_pre, preferred_element_type=jnp.float32
    )
    up_local = jnp.einsum("ecd,ecf->edf", expert_in, d_up_pre, preferred_element_type=jnp.float32)
    d_expert_in = (
        jnp.einsum("ecf,edf->ecd", d_gate_pre, gate_back, preferred_element_type=jnp.float32)
        + jnp.einsum("ecf,edf->ecd", d_up_pre, up_back, preferred_element_type=jnp.float32)
    ).astype(jnp.bfloat16)
    d_returned = lax.all_to_all(d_expert_in, "ctx", split_axis=1, concat_axis=0, tiled=True)
    gate_grad, up_grad, down_grad = (
        lax.psum_scatter(
            gate_local.astype(jnp.bfloat16), "fsdp", scatter_dimension=1, tiled=True
        ).astype(jnp.float32),
        lax.psum_scatter(
            up_local.astype(jnp.bfloat16), "fsdp", scatter_dimension=1, tiled=True
        ).astype(jnp.float32),
        lax.psum_scatter(
            down_local.astype(jnp.bfloat16), "fsdp", scatter_dimension=1, tiled=True
        ).astype(jnp.float32),
    )
    d_normed_two = jnp.sum(pick_rows(d_returned).astype(jnp.float32), axis=1)
    gate_mean = jnp.sum(gates * gate_grad_k, axis=-1, keepdims=True)
    d_chosen = gates * (gate_grad_k - gate_mean)
    d_logits = jnp.sum(route_hot * d_chosen[..., None], axis=1).astype(jnp.bfloat16)
    router_local = jnp.dot(normed_two.T, d_logits, preferred_element_type=jnp.float32)
    d_normed_two = d_normed_two + jnp.dot(
        d_logits, router_back.T, preferred_element_type=jnp.float32
    )
    _, norm_two_back = jax.vjp(rms_scale, mid_rows, gain_ffn)
    d_mid_norm, gain_ffn_local = norm_two_back(d_normed_two)
    d_mid = grad_rows + d_mid_norm
    d_proj = d_mid.astype(jnp.bfloat16)
    output_local = jnp.dot(attn_rows.T, d_proj, preferred_element_type=jnp.float32)
    d_attn = jnp.dot(d_proj, output_back.T, preferred_element_type=jnp.float32).astype(jnp.bfloat16)
    d_attn_four = d_attn.reshape(tok_rows, KVH, group_size, HD)
    delta_rows = jnp.einsum(
        "rkgd,rkgd->kgr",
        d_attn_four,
        attn_rows.reshape(tok_rows, KVH, group_size, HD),
        preferred_element_type=jnp.float32,
    )

    def backward_block(d_query, pieces):
        key_piece, value_piece, pos_piece = pieces
        scores = block_scores(query_four, key_piece, pos_piece, query_pos, score_scale)
        weights = jnp.exp(scores - log_total[..., None])
        d_value = jnp.einsum(
            "kgrc,rkgd->ckd",
            weights.astype(jnp.bfloat16),
            d_attn_four,
            preferred_element_type=jnp.float32,
        )
        d_weights = jnp.einsum(
            "rkgd,ckd->kgrc", d_attn_four, value_piece, preferred_element_type=jnp.float32
        )
        d_scores = (weights * (d_weights - delta_rows[..., None]) * score_scale).astype(
            jnp.bfloat16
        )
        d_query = d_query + jnp.einsum(
            "kgrc,ckd->rkgd", d_scores, key_piece, preferred_element_type=jnp.float32
        )
        d_key = jnp.einsum(
            "kgrc,rkgd->ckd", d_scores, query_four, preferred_element_type=jnp.float32
        )
        return (d_query, (d_key, d_value))

    d_query, (key_parts, value_parts) = lax.scan(
        backward_block,
        jnp.zeros((tok_rows, KVH, group_size, HD), jnp.float32),
        (split_blocks(keys_back), split_blocks(values_back), pos_blocks),
    )
    key_sum, value_sum = (
        lax.psum_scatter(
            key_parts.reshape(key_count, KVH * HD).astype(jnp.bfloat16),
            "ctx",
            scatter_dimension=0,
            tiled=True,
        ).astype(jnp.float32),
        lax.psum_scatter(
            value_parts.reshape(key_count, KVH * HD).astype(jnp.bfloat16),
            "ctx",
            scatter_dimension=0,
            tiled=True,
        ).astype(jnp.float32),
    )
    d_query_low = (
        unrotate(d_query.reshape(tok_rows, H, HD), cos_table, sin_table)
        .reshape(tok_rows, H * HD)
        .astype(jnp.bfloat16)
    )
    d_key_low = (
        unrotate(key_sum.reshape(tok_rows, KVH, HD), cos_table, sin_table)
        .reshape(tok_rows, KVH * HD)
        .astype(jnp.bfloat16)
    )
    d_value_low = value_sum.astype(jnp.bfloat16)
    query_local = jnp.dot(normed_one.T, d_query_low, preferred_element_type=jnp.float32)
    key_local = jnp.dot(normed_one.T, d_key_low, preferred_element_type=jnp.float32)
    value_local = jnp.dot(normed_one.T, d_value_low, preferred_element_type=jnp.float32)
    d_normed_one = (
        jnp.dot(d_query_low, query_back.T, preferred_element_type=jnp.float32)
        + jnp.dot(d_key_low, key_back.T, preferred_element_type=jnp.float32)
        + jnp.dot(d_value_low, value_back.T, preferred_element_type=jnp.float32)
    )
    _, norm_one_back = jax.vjp(rms_scale, x_rows, gain_attn)
    d_x_norm, gain_attn_local = norm_one_back(d_normed_one)
    in_grad = (d_mid + d_x_norm)[None]
    attn_gain_grad, ffn_gain_grad, query_grad, key_grad, value_grad, output_grad, router_grad = (
        lax.psum_scatter(gain_attn_local, ("ctx", "fsdp"), scatter_dimension=0, tiled=True),
        lax.psum_scatter(gain_ffn_local, ("ctx", "fsdp"), scatter_dimension=0, tiled=True),
        lax.psum_scatter(query_local, ("ctx", "fsdp"), scatter_dimension=0, tiled=True),
        lax.psum_scatter(key_local, ("ctx", "fsdp"), scatter_dimension=0, tiled=True),
        lax.psum_scatter(value_local, ("ctx", "fsdp"), scatter_dimension=0, tiled=True),
        lax.psum_scatter(output_local, ("ctx", "fsdp"), scatter_dimension=0, tiled=True),
        lax.psum_scatter(router_local, ("ctx", "fsdp"), scatter_dimension=0, tiled=True),
    )
    return (
        block_out[None],
        in_grad,
        attn_gain_grad,
        ffn_gain_grad,
        query_grad,
        key_grad,
        value_grad,
        output_grad,
        router_grad,
        gate_grad,
        up_grad,
        down_grad,
    )


BF16 = jnp.bfloat16
F32 = jnp.float32
HEADS_OUT = H // KVH
QCOLS = HEADS_OUT * HD
VMEM_LIMIT = 60 * 1024 * 1024


def dot32(left, right, dims=((1,), (0,))):
    return lax.dot_general(left, right, (dims, ((), ())), preferred_element_type=F32)


def swap(values, bit):
    return lax.ppermute(values, "fsdp", [(i, i ^ bit) for i in range(KVH)])


def shift(values, step):
    count = lax.axis_size("ctx")
    return lax.ppermute(values, "ctx", [(i, (i + step) % count) for i in range(count)])


def plane_gather(rows):
    half = rows.shape[0] // 2
    low, high = rows[:half], rows[half:]
    low_x, high_y = swap(low, 2), swap(high, 4)
    low_pair = jnp.stack([low, low_x])
    high_pair = jnp.stack([high, high_y])
    low_far, high_far = swap(low_pair, 4), swap(high_pair, 2)
    quad = jnp.stack(
        [
            jnp.concatenate([low, high], axis=0),
            jnp.concatenate([low_x, high_far[0]], axis=0),
            jnp.concatenate([low_far[0], high_y], axis=0),
            jnp.concatenate([low_far[1], high_far[1]], axis=0),
        ]
    )
    other = swap(quad, 1)
    return jnp.stack([quad, other], axis=1).reshape((KVH,) + rows.shape)


def plane_scatter(parts):
    rows, width = parts.shape[1:]
    half = rows // 2
    grid = parts.reshape(4, 2, rows, width)
    quad = grid[:, 0].astype(F32) + swap(grid[:, 1], 1).astype(F32)
    quad = quad.astype(BF16).reshape(2, 2, rows, width)
    low, high = quad[:, :, :half], quad[:, :, half:]
    low_in = swap(low[:, 1], 2)
    high_in = swap(high[1], 4)
    low_sum = (low[:, 0].astype(F32) + low_in.astype(F32)).astype(BF16)
    high_sum = (high[0].astype(F32) + high_in.astype(F32)).astype(BF16)
    low_last = swap(low_sum[1], 4)
    high_last = swap(high_sum[1], 2)
    return jnp.concatenate(
        [
            low_sum[0].astype(F32) + low_last.astype(F32),
            high_sum[0].astype(F32) + high_last.astype(F32),
        ],
        axis=0,
    )


def small_gather(rows):
    pair = jnp.stack([rows, swap(rows, 1)])
    quad = jnp.concatenate([pair, swap(pair, 2)], axis=0)
    return jnp.concatenate([quad, swap(quad, 4)], axis=0)


def pick(stacked, index):
    return lax.dynamic_index_in_dim(stacked, index, axis=0, keepdims=False)


def attn_forward(q_ref, kv0, kv1, kv2, kv3, bias_ref, o_ref, lse_ref, *, scale):
    keys = jnp.concatenate([kv[0, :, :HD] for kv in (kv0, kv1, kv2, kv3)], axis=0)
    values = jnp.concatenate([kv[0, :, HD:] for kv in (kv0, kv1, kv2, kv3)], axis=0)
    outs, logs = [], []
    for g in range(HEADS_OUT):
        query = q_ref[0, :, g * HD : (g + 1) * HD]
        scores = dot32(query, keys, ((1,), (1,))) * scale + bias_ref[...]
        top = jnp.max(scores, axis=-1, keepdims=True)
        total = jnp.sum(jnp.exp(scores - top), axis=-1, keepdims=True)
        log_total = top + jnp.log(total)
        weights = jnp.exp(scores - log_total).astype(BF16)
        outs.append(dot32(weights, values))
        logs.append(log_total)
    o_ref[0] = jnp.concatenate(outs, axis=-1).astype(BF16)
    lse_ref[0] = jnp.concatenate(logs, axis=-1)


def attn_backward(
    q_ref, kv0, kv1, kv2, kv3, do_ref, o_ref, lse_ref, bias_ref, cos_ref, sin_ref,
    dq_ref, dkv0, dkv1, dkv2, dkv3, *, scale
):
    keys = jnp.concatenate([kv[0, :, :HD] for kv in (kv0, kv1, kv2, kv3)], axis=0)
    values = jnp.concatenate([kv[0, :, HD:] for kv in (kv0, kv1, kv2, kv3)], axis=0)
    cos, sin = cos_ref[...], sin_ref[...]
    d_key = d_value = None
    d_query = []
    for g in range(HEADS_OUT):
        cols = slice(g * HD, (g + 1) * HD)
        query, d_out, out = q_ref[0, :, cols], do_ref[0, :, cols], o_ref[0, :, cols]
        scores = dot32(query, keys, ((1,), (1,))) * scale + bias_ref[...]
        weights = jnp.exp(scores - lse_ref[0, :, g : g + 1])
        delta = jnp.sum(d_out.astype(F32) * out.astype(F32), axis=-1, keepdims=True)
        d_weights = dot32(d_out, values, ((1,), (1,)))
        d_scores = (weights * (d_weights - delta) * scale).astype(BF16)
        dq = dot32(d_scores, keys)
        first, second = dq[:, : HD // 2], dq[:, HD // 2 :]
        d_query += [first * cos + second * sin, second * cos - first * sin]
        dk = dot32(d_scores, query, ((0,), (0,)))
        dv = dot32(weights.astype(BF16), d_out, ((0,), (0,)))
        d_key = dk if d_key is None else d_key + dk
        d_value = dv if d_value is None else d_value + dv
    dq_ref[0] = jnp.concatenate(d_query, axis=-1).astype(BF16)
    both = jnp.concatenate([d_key, d_value], axis=-1).astype(BF16)
    rows = both.shape[0] // 4
    for index, ref in enumerate((dkv0, dkv1, dkv2, dkv3)):
        ref[0] = both[index * rows : (index + 1) * rows]


def expert_main(base_ref, x_ref, g_ref, gate_ref, wg_ref, wu_ref, wd_ref,
                eo_ref, dx_ref, hid_ref, dgu_ref, duu_ref):
    shape = x_ref.shape
    rows = shape[0] * shape[1]
    x = x_ref[...].reshape(rows, shape[2])
    grad = g_ref[...].reshape(rows, shape[2])
    w_gate, w_up, w_down = wg_ref[0], wu_ref[0], wd_ref[0]
    gate = gate_ref[0]
    gate_pre = dot32(x, w_gate)
    up_pre = dot32(x, w_up)
    sigma = 1.0 / (1.0 + jnp.exp(-gate_pre))
    silu = gate_pre * sigma
    hidden = silu * up_pre
    back = dot32(grad, w_down, ((1,), (1,)))
    d_gate = jnp.sum(hidden * back, axis=-1, keepdims=True)
    gated = (hidden * gate).astype(BF16)
    eo_ref[...] = dot32(gated, w_down).astype(BF16).reshape(eo_ref.shape)
    d_hidden = back * gate
    d_gate_pre = (d_hidden * up_pre * (sigma * (1.0 + gate_pre * (1.0 - sigma)))).astype(BF16)
    d_up_pre = (d_hidden * silu).astype(BF16)
    d_rows = dot32(d_gate_pre, w_gate, ((1,), (1,))) + dot32(d_up_pre, w_up, ((1,), (1,)))
    dx_ref[:, :, : shape[2]] = d_rows.astype(BF16).reshape(shape)
    extra = dx_ref.shape[2] - shape[2]
    lane = lax.broadcasted_iota(jnp.int32, (rows, extra), 1)
    here = base_ref[0] + pl.program_id(0)
    dx_ref[:, :, shape[2] :] = (
        jnp.where(lane == here, d_gate, 0.0).astype(BF16).reshape(shape[0], shape[1], extra)
    )
    hid_ref[0] = gated
    dgu_ref[0] = d_gate_pre
    duu_ref[0] = d_up_pre


def expert_grads(x_ref, g_ref, hid_ref, dgu_ref, duu_ref, dwg_ref, dwu_ref, dwd_ref):
    shape = x_ref.shape
    rows = shape[0] * shape[1]
    x = x_ref[...].reshape(rows, shape[2])
    grad = g_ref[...].reshape(rows, shape[2])
    dwg_ref[0] = dot32(x, dgu_ref[0], ((0,), (0,))).astype(BF16)
    dwu_ref[0] = dot32(x, duu_ref[0], ((0,), (0,))).astype(BF16)
    dwd_ref[0] = dot32(hid_ref[0], grad, ((0,), (0,))).astype(BF16)


def fast_body(
    hidden_in, out_grad, attn_gain, ffn_gain, w_query, w_key, w_value, w_output, w_router,
    w_gate, w_up, w_down, expert_ids,
):
    ctx_count = lax.axis_size("ctx")
    ctx_index = lax.axis_index("ctx")
    me = lax.axis_index("fsdp")
    core, x_bit = me % 2, (me // 2) % 2
    rows, width = hidden_in.shape[1:]
    half_rows = rows // 2
    depth = w_query.shape[0]
    experts, hid_width = w_gate.shape[0], w_gate.shape[2]
    served = experts // 2
    half_hid = hid_width // 2
    hid_part = w_down.shape[1]
    scale = HD ** (-0.5)
    relative = me ^ jnp.arange(KVH, dtype=jnp.int32)
    call = functools.partial(
        pl.pallas_call, compiler_params=pltpu.CompilerParams(vmem_limit_bytes=VMEM_LIMIT)
    )

    seqs = plane_gather(hidden_in[0])
    small = small_gather(
        jnp.concatenate([w_router, attn_gain[:, None], ffn_gain[:, None]], axis=1)
    )
    small = jnp.take(small, relative, axis=0).reshape(width, E + 2)
    router_full = small[:, :E]
    gain_attn = small[:, E].astype(F32)
    gain_ffn = small[:, E + 1].astype(F32)
    own_cols = jnp.concatenate(
        [
            w_query.reshape(depth, KVH, QCOLS),
            w_key.reshape(depth, KVH, HD),
            w_value.reshape(depth, KVH, HD),
        ],
        axis=2,
    ).transpose(1, 0, 2)
    w_heads = lax.all_to_all(own_cols, "fsdp", split_axis=0, concat_axis=0, tiled=True)
    w_heads = w_heads.reshape(width, QCOLS + 2 * HD)

    def half_cols(which):
        col = jnp.arange(half_hid, dtype=jnp.int32)
        span = hid_part // 2
        source = hid_part * (col // span) + span * which + col % span
        return (jnp.arange(hid_width, dtype=jnp.int32)[:, None] == source[None, :]).astype(BF16)

    keep_cols, send_cols = half_cols(core), half_cols(1 - core)

    def by_side(weights):
        halves = weights.reshape((2, served) + weights.shape[1:])
        return pick(halves, x_bit), pick(halves, 1 - x_bit)

    def expert_parts(mine, theirs):
        other = [swap(part, 1) for part in theirs]
        near = [mine[0], other[0]]
        near += [swap(part, 2) for part in (mine[1], other[1])]
        far = [swap(part, 4) for part in near]
        return jnp.take(jnp.stack(near + far), relative, axis=0)

    def split_in(weights):
        sides = by_side(weights)
        return (
            [jnp.einsum("edf,fq->edq", s, keep_cols, preferred_element_type=BF16) for s in sides],
            [jnp.einsum("edf,fq->edq", s, send_cols, preferred_element_type=BF16) for s in sides],
        )

    def split_down(weights):
        sides = by_side(weights.reshape(experts, 2, hid_part // 2, width))
        return (
            [lax.dynamic_index_in_dim(s, core, axis=1, keepdims=False) for s in sides],
            [lax.dynamic_index_in_dim(s, 1 - core, axis=1, keepdims=False) for s in sides],
        )

    gate_w = expert_parts(*split_in(w_gate)).transpose(1, 0, 2, 3).reshape(served, width, half_hid)
    up_w = expert_parts(*split_in(w_up)).transpose(1, 0, 2, 3).reshape(served, width, half_hid)
    down_w = expert_parts(*split_down(w_down)).transpose(1, 0, 2, 3).reshape(
        served, half_hid, width
    )

    def pair_gather(values):
        blocks = []
        for step in range(ctx_count):
            here = shift(values, step) if step else values
            pair = jnp.stack([here, swap(here, 2)])
            blocks += [pair, swap(pair, 1)]
        return jnp.concatenate(blocks, axis=0)

    def pair_scatter(parts):
        total = None
        for step in reversed(range(ctx_count)):
            grid = parts[step]
            pair = (grid[0].astype(F32) + swap(grid[1], 1).astype(F32)).astype(BF16)
            one = pair[0].astype(F32) + swap(pair[1], 2).astype(F32)
            if step:
                one = shift(one.astype(BF16), -step).astype(F32)
            total = one if total is None else total + one
        return total

    grad_pair = pair_gather(out_grad[0])
    ids_pair = pair_gather(expert_ids[0].T)

    flat = seqs.reshape(KVH * rows, width)
    normed_all = rms_scale(flat.astype(F32), gain_attn).astype(BF16)
    query_pos = mirrored_positions(rows, half_rows, ctx_count, ctx_index)
    cos_table, sin_table = rope_tables(query_pos, HD)
    projected = jnp.dot(normed_all, w_heads, preferred_element_type=F32)
    heads = projected[:, : QCOLS + HD].reshape(KVH, rows, HEADS_OUT + 1, HD)
    rotated = rotate(heads, cos_table, sin_table).astype(BF16)
    query = rotated[:, :, :HEADS_OUT].reshape(KVH, rows, QCOLS)
    kv_own = jnp.concatenate(
        [
            rotated[:, :, HEADS_OUT],
            projected[:, QCOLS + HD :].astype(BF16).reshape(KVH, rows, HD),
        ],
        axis=-1,
    )
    kv_all = [kv_own] + [shift(kv_own, step) for step in range(1, ctx_count)]
    key_pos = jnp.concatenate(
        [
            mirrored_positions(rows, half_rows, ctx_count, (ctx_index - step) % ctx_count)
            for step in range(ctx_count)
        ]
    )
    bias = jnp.where(key_pos[None, :] <= query_pos[:, None], 0.0, NEG_FILL).astype(F32)
    seq_spec = lambda cols: pl.BlockSpec((1, rows, cols), lambda s: (s, 0, 0))
    whole = lambda *shape: pl.BlockSpec(shape, lambda s: (0,) * len(shape))
    kv_spec = [seq_spec(2 * HD)] * ctx_count
    attn_out, log_total = call(
        functools.partial(attn_forward, scale=scale),
        grid=(KVH,),
        in_specs=[seq_spec(QCOLS)] + kv_spec + [whole(rows, ctx_count * rows)],
        out_specs=[seq_spec(QCOLS), seq_spec(HEADS_OUT)],
        out_shape=[
            jax.ShapeDtypeStruct((KVH, rows, QCOLS), BF16),
            jax.ShapeDtypeStruct((KVH, rows, HEADS_OUT), F32),
        ],
        name="attn_forward",
    )(query, *kv_all, bias)
    attn_flat = attn_out.reshape(KVH * rows, QCOLS)
    mixed = jnp.dot(attn_flat, w_output, preferred_element_type=F32).astype(BF16)
    x_rows = hidden_in[0].astype(F32)
    mid_rows = x_rows + plane_scatter(mixed.reshape(KVH, rows, width))
    normed_two = rms_scale(mid_rows, gain_ffn).astype(BF16)

    tokens = pair_gather(normed_two)
    blocks = tokens.shape[0]
    expert_range = jnp.arange(E, dtype=jnp.int32)
    first_expert = ctx_index * experts + x_bit * served
    hot = jnp.any(ids_pair[:, :, None, :] == expert_range[None, None, :, None], axis=1)
    own_hot = lax.dynamic_slice_in_dim(hot, first_expert, served, axis=1)
    upper = (jnp.arange(rows)[:, None] <= jnp.arange(rows)[None, :]).astype(BF16)
    slots = jnp.einsum(
        "bet,tu->beu", own_hot.astype(BF16), upper, preferred_element_type=F32
    ).astype(jnp.int32) - 1
    slots = jnp.where(own_hot, slots, -1)
    choose = (slots[:, :, None, :] == jnp.arange(CAP, dtype=jnp.int32)[None, None, :, None])
    choose = choose.astype(BF16).reshape(blocks, served * CAP, rows)
    logits = jnp.einsum("btd,de->bet", tokens, router_full, preferred_element_type=F32)
    masked = jnp.where(hot, logits, NEG_FILL)
    raised = jnp.where(hot, jnp.exp(masked - jnp.max(masked, axis=1, keepdims=True)), 0.0)
    gates_t = raised / jnp.sum(raised, axis=1, keepdims=True)
    own_gates = lax.dynamic_slice_in_dim(gates_t, first_expert, served, axis=1)
    slot_gates = jnp.sum(
        choose.reshape(blocks, served, CAP, rows).astype(F32) * own_gates[:, :, None, :], axis=-1
    )
    slot_gates = slot_gates.transpose(1, 0, 2).reshape(served, blocks * CAP, 1)
    expert_x = jnp.einsum("bst,btd->bsd", choose, tokens, preferred_element_type=BF16)
    expert_g = jnp.einsum("bst,btd->bsd", choose, grad_pair, preferred_element_type=BF16)
    slot_rows = blocks * CAP
    wide = width + 128
    act_spec = lambda cols: pl.BlockSpec((blocks, CAP, cols), lambda e, *_: (0, e, 0))
    per_expert = lambda a, b: pl.BlockSpec((1, a, b), lambda e, *_: (e, 0, 0))
    hid_shape = jax.ShapeDtypeStruct((served, slot_rows, half_hid), BF16)
    eo, dx, gated, d_gu, d_uu = call(
        expert_main,
        grid_spec=pltpu.PrefetchScalarGridSpec(
            num_scalar_prefetch=1,
            grid=(served,),
            in_specs=[
                act_spec(width),
                act_spec(width),
                per_expert(slot_rows, 1),
                per_expert(width, half_hid),
                per_expert(width, half_hid),
                per_expert(half_hid, width),
            ],
            out_specs=[
                act_spec(width),
                act_spec(wide),
                per_expert(slot_rows, half_hid),
                per_expert(slot_rows, half_hid),
                per_expert(slot_rows, half_hid),
            ],
        ),
        out_shape=[
            jax.ShapeDtypeStruct((blocks, served * CAP, width), BF16),
            jax.ShapeDtypeStruct((blocks, served * CAP, wide), BF16),
            hid_shape,
            hid_shape,
            hid_shape,
        ],
        name="expert_main",
    )(first_expert[None], expert_x, expert_g, slot_gates, gate_w, up_w, down_w)
    d_tokens = jnp.einsum("bst,bsd->btd", choose, dx, preferred_element_type=BF16)
    dx_total = pair_scatter(d_tokens.reshape(ctx_count, 2, 2, rows, wide))
    grads_w = call(
        expert_grads,
        grid=(served,),
        in_specs=[act_spec(width)] * 2 + [per_expert(slot_rows, half_hid)] * 3,
        out_specs=[
            per_expert(width, half_hid),
            per_expert(width, half_hid),
            per_expert(half_hid, width),
        ],
        out_shape=[
            jax.ShapeDtypeStruct((served, width, half_hid), BF16),
            jax.ShapeDtypeStruct((served, width, half_hid), BF16),
            jax.ShapeDtypeStruct((served, half_hid, width), BF16),
        ],
        name="expert_grads",
    )(expert_x, expert_g, gated, d_gu, d_uu)
    outs = jnp.einsum("bst,bsd->btd", choose, eo, preferred_element_type=BF16)
    mixture = pair_scatter(outs.reshape(ctx_count, 2, 2, rows, width))
    block_out = (mid_rows + mixture).astype(BF16)

    d_gates = dx_total[:, width : width + E]
    gates = gates_t[0].T
    d_logits = (gates * (d_gates - jnp.sum(gates * d_gates, axis=-1, keepdims=True))).astype(BF16)
    router_local = jnp.dot(normed_two.T, d_logits, preferred_element_type=F32)
    d_normed_two = dx_total[:, :width] + jnp.dot(
        d_logits, router_full.T, preferred_element_type=F32
    )
    _, norm_two_back = jax.vjp(rms_scale, mid_rows, gain_ffn)
    d_mid_norm, gain_ffn_local = norm_two_back(d_normed_two)
    d_mid = out_grad[0].astype(F32) + d_mid_norm

    d_proj_all = plane_gather(d_mid.astype(BF16)).reshape(KVH * rows, width)
    d_attn = jnp.dot(d_proj_all, w_output.T, preferred_element_type=F32).astype(BF16)
    output_part = jnp.dot(attn_flat.T, d_proj_all, preferred_element_type=F32).astype(BF16)
    back = call(
        functools.partial(attn_backward, scale=scale),
        grid=(KVH,),
        in_specs=[seq_spec(QCOLS)]
        + kv_spec
        + [seq_spec(QCOLS), seq_spec(QCOLS), seq_spec(HEADS_OUT), whole(rows, ctx_count * rows)]
        + [whole(rows, HD // 2)] * 2,
        out_specs=[seq_spec(QCOLS)] + kv_spec,
        out_shape=[jax.ShapeDtypeStruct((KVH, rows, QCOLS), BF16)]
        + [jax.ShapeDtypeStruct((KVH, rows, 2 * HD), BF16)] * ctx_count,
        name="attn_backward",
    )(
        query, *kv_all, d_attn.reshape(KVH, rows, QCOLS), attn_out, log_total, bias,
        cos_table[:, 0], sin_table[:, 0],
    )
    d_query = back[0].reshape(KVH * rows, QCOLS)
    kv_sum = back[1].astype(F32)
    for step in range(1, ctx_count):
        kv_sum = kv_sum + shift(back[1 + step], -step).astype(F32)
    d_key = unrotate(kv_sum[:, :, None, :HD], cos_table, sin_table)[:, :, 0]
    d_kv = jnp.concatenate([d_key, kv_sum[:, :, HD:]], axis=-1).astype(BF16)
    d_kv = d_kv.reshape(KVH * rows, 2 * HD)
    d_heads = jnp.concatenate([d_query, d_kv], axis=-1)
    d_normed = jnp.dot(d_heads, w_heads.T, preferred_element_type=F32)
    gain_attn_part = jnp.sum(
        d_normed * rms_scale(flat.astype(F32), jnp.ones((), F32)), axis=0
    )
    d_normed_one = plane_scatter(d_normed.astype(BF16).reshape(KVH, rows, width))
    _, norm_one_back = jax.vjp(rms_scale, x_rows, gain_attn)
    d_x_norm, _ = norm_one_back(d_normed_one)
    in_grad = (d_mid + d_x_norm)[None]

    def ctx_scatter(parts):
        total = pick(parts, ctx_index).astype(F32)
        for step in range(1, ctx_count):
            block = pick(parts, (ctx_index + step) % ctx_count)
            total = total + shift(block, step).astype(F32)
        return total

    def plane_exchange(parts):
        mine = jnp.take(parts, relative, axis=0)
        got = [mine[0]] + [
            lax.ppermute(mine[m], "fsdp", [(i, i ^ m) for i in range(KVH)]) for m in range(1, KVH)
        ]
        return jnp.take(jnp.stack(got), relative, axis=0)

    def rows_to_owner(local):
        out_rows = local.shape[0] // (ctx_count * KVH)
        mine = ctx_scatter(local.reshape(ctx_count, KVH, out_rows, local.shape[1]))
        return plane_exchange(mine.astype(BF16)).astype(F32)

    head_part = jnp.dot(normed_all.T, d_heads, preferred_element_type=F32)
    stats = jnp.concatenate(
        [
            head_part,
            gain_attn_part[:, None],
            gain_ffn_local[:, None],
            router_local,
        ],
        axis=1,
    ).astype(BF16)
    got = rows_to_owner(stats)
    cols = QCOLS + 2 * HD
    query_grad = got[:, :, :QCOLS].transpose(1, 0, 2).reshape(-1, H * HD)
    key_grad = got[:, :, QCOLS : QCOLS + HD].transpose(1, 0, 2).reshape(-1, KVH * HD)
    value_grad = got[:, :, QCOLS + HD : cols].transpose(1, 0, 2).reshape(-1, KVH * HD)
    shared = jnp.sum(got[:, :, cols:], axis=0)
    attn_gain_grad, ffn_gain_grad, router_grad = shared[:, 0], shared[:, 1], shared[:, 2:]
    output_mine = ctx_scatter(output_part.reshape(ctx_count, -1, width)).astype(BF16)
    route = []
    for c in range(ctx_count):
        for j in range(KVH):
            block = j * ctx_count + c
            route.append((c * KVH + j, block))
    output_grad = lax.ppermute(output_mine, ("ctx", "fsdp"), route).astype(F32)

    def expert_back(grad_rel):
        far = [swap(grad_rel[m], 4) for m in range(4, 8)]
        near = [(grad_rel[m].astype(F32) + far[m].astype(F32)).astype(BF16) for m in range(4)]
        other = [swap(near[2], 2), swap(near[3], 2)]
        sides = []
        for m in range(2):
            both = jnp.stack([near[m], other[m]])
            sides.append(jnp.take(both, x_bit ^ jnp.arange(2), axis=0).reshape(
                (experts,) + near[m].shape[1:]))
        return sides[0], swap(sides[1], 1)

    def back_in(grad):
        parts = grad.reshape(served, KVH, depth, half_hid).transpose(1, 0, 2, 3)
        own, other = expert_back(jnp.take(parts, relative, axis=0))
        return jnp.einsum(
            "edq,fq->edf", own, keep_cols, preferred_element_type=F32
        ) + jnp.einsum("edq,fq->edf", other, send_cols, preferred_element_type=F32)

    def back_down(grad):
        parts = grad.reshape(served, KVH, hid_part // 2, width).transpose(1, 0, 2, 3)
        own, other = expert_back(jnp.take(parts, relative, axis=0))
        both = jnp.take(jnp.stack([own, other], axis=1), core ^ jnp.arange(2), axis=1)
        return both.reshape(experts, hid_part, width).astype(F32)

    gate_grad, up_grad, down_grad = back_in(grads_w[0]), back_in(grads_w[1]), back_down(grads_w[2])
    return (
        block_out[None],
        in_grad,
        attn_gain_grad,
        ffn_gain_grad,
        query_grad,
        key_grad,
        value_grad,
        output_grad,
        router_grad,
        gate_grad,
        up_grad,
        down_grad,
    )


def solution(mesh):
    body = fast_body if mesh.shape["fsdp"] == KVH else wide_body
    return jax.shard_map(
        body,
        mesh=mesh,
        in_specs=(
            P("fsdp", "ctx", None),
            P("fsdp", "ctx", None),
            P("fsdp"),
            P("fsdp"),
            P("fsdp", None),
            P("fsdp", None),
            P("fsdp", None),
            P("fsdp", None),
            P("fsdp", None),
            P("ctx", "fsdp", None),
            P("ctx", "fsdp", None),
            P("ctx", "fsdp", None),
            P("fsdp", "ctx", None),
        ),
        out_specs=(
            P("fsdp", "ctx", None),
            P("fsdp", "ctx", None),
            P(("ctx", "fsdp")),
            P(("ctx", "fsdp")),
            P(("ctx", "fsdp"), None),
            P(("ctx", "fsdp"), None),
            P(("ctx", "fsdp"), None),
            P(("ctx", "fsdp"), None),
            P(("ctx", "fsdp"), None),
            P("ctx", "fsdp", None),
            P("ctx", "fsdp", None),
            P("ctx", "fsdp", None),
        ),
        check_vma=False,
    )
```
